32 devices in a mesh: blk: 16 (over z, y, x), tok: 2 (over core).
Axes of the slice: x: 2, y: 2, z: 4, core: 2. Of those that a mesh axis runs over, the one named last changes fastest.
Arguments:
- tokens: bfloat16 [512, 9216], P(('tok', 'blk')), parts along dimension 0, may hold values from -6 to 6
- block_ids: int32 [512, 2], P(('tok', 'blk')), parts along dimension 0, may hold values from 0 to 15, all different within a row; in each aligned block of 16 rows (0 to 15, 16 to 31, ...) at most 5 rows name the same one
- w_in: bfloat16 [9216, 2048], P(None, 'blk'), may hold values from -0.0625 to 0.0625
- bias_in: float32 [2048], P('blk'), may hold values from -3 to 3
- w_out: bfloat16 [2048, 9216], P('blk'), may hold values from -0.375 to 0.375
Outputs:
- ffn_out: bfloat16 [512, 9216], P(('tok', 'blk')), parts along dimension 0
The draws below stay inside these ranges and needn't reach their ends.
There are 2 independent parts, one for each index of `tok`. The reference program is written for one: setup_inputs(seed, part) draws one part's arguments, and reference() takes and returns one part's arrays. A program takes and returns all parts, laid end to end along the dimension named above; an argument that names none is the same for every part. Nothing has to cross between parts.
Inputs may be any that keep to these rules, and one draw needn't show every extreme that they name: `block_ids`: each row names 2 different blocks. Among the 16 rows of one device no block is named by more than 5 rows, and some block is named by exactly 5 of them.
All inputs are finite; a program needn't handle non-finite values.
Results may differ from the reference program's by a relative error of at most 0.0057.
Values may be sent and summed in bfloat16 or wider, within the bound.
A program may use at most 128 MiB of HBM per device.

```python
import math
import jax
import jax.numpy as jnp
import numpy as np
from jax import lax

D = 9216
BLOCK = 128
TOK_DEV = 16
BLOCKS = 16
TOPK = 2
CAP = 5
TOKENS = 256


def levels(key, extent, cuts, least, largest):
    level = 1.0
    for position, parts in cuts:
        draws = jax.random.uniform(jax.random.fold_in(jax.random.fold_in(key, 6), position), (parts,), jnp.float32, least / len(cuts), largest / len(cuts))
        level = level * jnp.repeat(jnp.exp(draws), extent[position] // parts).reshape((-1,) + (1,) * (len(extent) - 1 - position))
    return level


def assign_block(rng, own, number, rows, number_of, top, limit, slope):
    ranking = jax.random.permutation(rng, number_of)
    heavy_load, ordinary = shares(number_of, rows * top, limit, slope, True), shares(number_of, rows * top, limit, slope, False)
    places = jnp.arange(number_of)

    def named(lengths, turn):
        used = int((lengths > 0).sum())
        fixed = max(1, used // 4)
        passed = fixed + (places - fixed + turn * (used - fixed)) % max(1, number_of - fixed)
        return jnp.zeros((number_of,), jnp.int32).at[ranking[jnp.where(places < fixed, places, passed)]].set(jnp.asarray(lengths, jnp.int32))

    lengths = jnp.where(number % 4 == 0, named(heavy_load, number // 4), named(ordinary, number - number // 4 - 1))
    mixed = jax.random.permutation(jax.random.fold_in(own, 3), number_of)
    giver, taker = mixed[0:number_of // 2 * 2:2], mixed[1:number_of // 2 * 2:2]
    slack = jnp.minimum(lengths[giver] - 1, limit - lengths[taker]) // 2
    slack = jnp.where((giver == ranking[0]) | (taker == ranking[0]) | (lengths[taker] == 0), 0, jnp.maximum(slack, 0))
    passed = jax.random.randint(jax.random.fold_in(own, 4), (number_of // 2,), 0, 1 << 20) % (slack + 1)
    lengths = lengths.at[giver].add(-passed).at[taker].add(passed)
    members = jnp.searchsorted(jnp.cumsum(lengths), jnp.arange(rows * top), side="right").astype(jnp.int32)
    listing = members.reshape(top, rows).T
    listing = listing[jax.random.permutation(jax.random.fold_in(own, 1), rows)]
    turn = jax.random.randint(jax.random.fold_in(own, 2), (rows, 1), 0, top)
    return jnp.take_along_axis(listing, (jnp.arange(top)[None, :] + turn) % top, axis=1)


def shares(count, total, bound, skew, full):
    loads = [(1 << 20) // math.isqrt(standing ** skew) + 1 for standing in range(1, count + 1)]
    largest = bound if full else min(bound, max(-(-total // count), total * loads[0] // sum(loads)))
    least = 1 if total - largest >= count - 1 else 0
    counts, rest = [largest] + [least] * (count - 1), total - largest - least * (count - 1)
    while rest > 0:
        movable = [i for i in range(1, count) if counts[i] < largest] or [i for i in range(1, count) if counts[i] < bound]
        pool, budget = sum([loads[i] for i in movable]), rest
        for i in movable:
            more = min(bound - counts[i], max(1, budget * loads[i] // pool), rest)
            counts[i] = counts[i] + more
            rest = rest - more
    return np.array(counts)


def centred(key, shape, width, reach, shards=(), kind=jnp.bfloat16):
    values = width * jax.random.normal(key, shape, jnp.float32)
    if shards:
        values = values * levels(key, shape, shards, -0.22, 0.18)
    return jnp.clip(values, -reach, reach).astype(kind)


def setup_inputs(seed: int = 0, part: int = 0) -> dict:
    keys = jax.random.split(jax.random.key(seed), 6)
    part_keys = jax.random.split(jax.random.fold_in(keys[5], part), 6)
    tokens = centred(part_keys[0], (TOKENS, D), 1.0, 6.0, ((0, 16),))
    block_ids_keys = jax.random.split(jax.random.fold_in(part_keys[1], 1), TOKENS // TOK_DEV)
    block_ids_turns = jax.random.permutation(jax.random.fold_in(part_keys[1], 3), TOKENS // TOK_DEV)
    block_ids = jax.vmap(lambda own, number: assign_block(jax.random.fold_in(part_keys[1], 2), own, number, TOK_DEV, BLOCKS, TOPK, CAP, 2))(block_ids_keys, block_ids_turns).reshape((TOKENS, TOPK))
    w_in = centred(keys[2], (D, BLOCKS * BLOCK), D ** -0.5, 0.0625, ((1, 16),))
    bias_in = centred(keys[3], (BLOCKS * BLOCK,), 0.5, 3.0, ((0, 16),), jnp.float32)
    w_out = centred(keys[4], (BLOCKS * BLOCK, D), (TOPK * BLOCK) ** -0.5, 0.375, ((0, 16),))
    return {"tokens": tokens, "block_ids": block_ids, "w_in": w_in, "bias_in": bias_in, "w_out": w_out}


def reference(tokens, block_ids, w_in, bias_in, w_out):
    def one_block(total, index):
        start = (index * BLOCK).astype(jnp.int32)
        w_first = lax.dynamic_slice_in_dim(w_in, start, BLOCK, 1)
        b_first = lax.dynamic_slice_in_dim(bias_in, start, BLOCK, 0)
        w_second = lax.dynamic_slice_in_dim(w_out, start, BLOCK, 0)
        pre_act = jnp.dot(tokens, w_first, preferred_element_type=jnp.float32) + b_first.astype(jnp.float32)
        hidden = jnp.maximum(pre_act, 0.0).astype(jnp.bfloat16)
        contrib = jnp.dot(hidden, w_second, preferred_element_type=jnp.float32).astype(jnp.bfloat16).astype(jnp.float32)
        chosen = jnp.any(block_ids == index, axis=1)
        return total + jnp.where(chosen[:, None], contrib, jnp.zeros_like(contrib)), None

    start_total = jnp.zeros((TOKENS, D), jnp.float32)
    total, unused = lax.scan(one_block, start_total, jnp.arange(BLOCKS, dtype=jnp.int32))
    return total.astype(jnp.bfloat16)
```

```python
import functools
import math

import jax
import jax.numpy as jnp
from jax import lax
from jax.experimental import pallas as pl
from jax.experimental.pallas import tpu as pltpu
from jax.sharding import PartitionSpec as P

CAP = 5
PARTS = 8
F32 = jnp.float32
BF16 = jnp.bfloat16


def iota(shape, dim):
    return lax.broadcasted_iota(jnp.int32, shape, dim)


def kernel(
    n, group, tok_ref, ids_ref, w_in_ref, bias_ref, w_out_ref, out_ref,
    tok8, win8, wout8, outgoing, incoming, result, returned, route, acc,
    load_sem, fsend, frecv, bsend, brecv,
):
    me = lax.axis_index("blk")
    tok_dev, top = ids_ref.shape
    width = tok8.shape[1]
    neurons = w_in_ref.shape[1]
    lanes = 128 * ((n + 127) // 128)
    slab = CAP * PARTS
    rows = group * slab

    loads = []
    for h in range(PARTS):
        cols = pl.ds(h * width, width)
        loads.append(pltpu.make_async_copy(
            tok_ref.at[:, cols], tok8.at[pl.ds(h * tok_dev, tok_dev)], load_sem.at[0, h]))
        loads.append(pltpu.make_async_copy(
            w_in_ref.at[cols], win8.at[:, pl.ds(h * neurons, neurons)], load_sem.at[1, h]))
        loads.append(pltpu.make_async_copy(
            w_out_ref.at[:, cols], wout8.at[pl.ds(h * neurons, neurons)], load_sem.at[2, h]))
    for copy in loads[0::3] + loads[1::3] + loads[2::3]:
        copy.start()

    barrier = pltpu.get_barrier_semaphore()
    for k in range(1, n):
        pl.semaphore_signal(barrier, inc=1, device_id={"blk": lax.rem(me + k, n)},
                            device_id_type=pl.DeviceIdType.MESH)

    ids = ids_ref[...]
    block = iota((tok_dev, lanes), 1)
    member = jnp.zeros((tok_dev, lanes), F32)
    for k in range(top):
        member = member + (ids[:, k:k + 1] == block).astype(F32)
    lower = (iota((tok_dev, tok_dev), 1) < iota((tok_dev, tok_dev), 0)).astype(F32)
    rank = jnp.dot(lower, member, preferred_element_type=F32)
    rank = jnp.where(member > 0.5, rank, 99.0)
    rank8 = jnp.concatenate([rank] * PARTS, axis=0).astype(BF16)

    for copy in loads[0::3]:
        copy.wait()
    for g in range(n // group):
        row = iota((rows, lanes), 0)
        target = lax.rem(me + g * group + row // slab, n)
        pick = (target == iota((rows, lanes), 1)).astype(BF16)
        place = lax.dot_general(pick, rank8, (((1,), (1,)), ((), ())), preferred_element_type=F32)
        r = iota((rows, PARTS * tok_dev), 0) % slab
        c = iota((rows, PARTS * tok_dev), 1)
        chosen = (jnp.abs(place - (r % CAP).astype(F32)) < 0.5) & (r // CAP == c // tok_dev)
        chosen = chosen.astype(BF16)
        route[pl.ds(g * rows, rows), :] = chosen
        packed = jnp.dot(chosen, tok8[...], preferred_element_type=F32).astype(BF16)
        for i in range(group):
            outgoing[g * group + i] = packed[i * slab:(i + 1) * slab]
        if g == 0:
            pl.semaphore_wait(barrier, n - 1)
        for i in range(group):
            k = g * group + i
            if k > 0:
                pltpu.make_async_remote_copy(
                    src_ref=outgoing.at[k], dst_ref=incoming.at[k],
                    send_sem=fsend.at[k], recv_sem=frecv.at[k],
                    device_id={"blk": lax.rem(me + k, n)},
                    device_id_type=pl.DeviceIdType.MESH).start()

    for copy in loads[1::3] + loads[2::3]:
        copy.wait()
    ra, rb = iota((rows, rows), 0), iota((rows, rows), 1)
    same = ((ra // slab == rb // slab) & (ra % CAP == rb % CAP)).astype(F32)
    part = (iota((rows, PARTS * neurons), 0) % slab // CAP) == (
        iota((rows, PARTS * neurons), 1) // neurons)
    for g in range(n // group):
        slabs = []
        for i in range(group):
            k = g * group + i
            if k == 0:
                slabs.append(outgoing[0])
            else:
                pltpu.make_async_remote_copy(
                    src_ref=outgoing.at[k], dst_ref=incoming.at[k],
                    send_sem=fsend.at[k], recv_sem=frecv.at[k],
                    device_id={"blk": lax.rem(me + k, n)},
                    device_id_type=pl.DeviceIdType.MESH).wait_recv()
                slabs.append(incoming[k])
        x = jnp.concatenate(slabs, axis=0)
        wide = jnp.where(part, jnp.dot(x, win8[...], preferred_element_type=F32), 0.0)
        own = wide[:, :neurons]
        for h in range(1, PARTS):
            own = own + wide[:, h * neurons:(h + 1) * neurons]
        pre = jnp.dot(same, own, preferred_element_type=F32, precision=lax.Precision.HIGHEST)
        hidden = jnp.maximum(pre + bias_ref[...], 0.0)
        hidden8 = jnp.where(part, jnp.concatenate([hidden] * PARTS, axis=1), 0.0).astype(BF16)
        back = jnp.dot(hidden8, wout8[...], preferred_element_type=F32).astype(BF16)
        for i in range(group):
            k = g * group + i
            if k == 0:
                returned[0] = back[:slab]
            else:
                result[k] = back[i * slab:(i + 1) * slab]
        for i in range(group):
            k = g * group + i
            if k > 0:
                pltpu.make_async_remote_copy(
                    src_ref=result.at[k], dst_ref=returned.at[k],
                    send_sem=bsend.at[k], recv_sem=brecv.at[k],
                    device_id={"blk": lax.rem(me - k + n, n)},
                    device_id_type=pl.DeviceIdType.MESH).start()

    for g in range(n // group):
        slabs = []
        for i in range(group):
            k = g * group + i
            if k > 0:
                pltpu.make_async_remote_copy(
                    src_ref=result.at[k], dst_ref=returned.at[k],
                    send_sem=bsend.at[k], recv_sem=brecv.at[k],
                    device_id={"blk": lax.rem(me - k + n, n)},
                    device_id_type=pl.DeviceIdType.MESH).wait_recv()
            slabs.append(returned[k])
        y = jnp.concatenate(slabs, axis=0)
        total = lax.dot_general(route[pl.ds(g * rows, rows), :], y, (((0,), (0,)), ((), ())),
                                preferred_element_type=F32)
        if g == 0:
            acc[...] = total
        elif g < n // group - 1:
            acc[...] += total
        else:
            total = acc[...] + total
            for h in range(PARTS):
                out_ref[:, h * width:(h + 1) * width] = (
                    total[h * tok_dev:(h + 1) * tok_dev].astype(BF16))
    for k in range(1, n):
        pltpu.make_async_remote_copy(
            src_ref=outgoing.at[k], dst_ref=incoming.at[k],
            send_sem=fsend.at[k], recv_sem=frecv.at[k],
            device_id={"blk": lax.rem(me + k, n)},
            device_id_type=pl.DeviceIdType.MESH).wait_send()
        pltpu.make_async_remote_copy(
            src_ref=result.at[k], dst_ref=returned.at[k],
            send_sem=bsend.at[k], recv_sem=brecv.at[k],
            device_id={"blk": lax.rem(me - k + n, n)},
            device_id_type=pl.DeviceIdType.MESH).wait_send()


def body(tokens, block_ids, w_in, bias_in, w_out):
    n = lax.axis_size("blk")
    tok_dev, model_width = tokens.shape
    neurons = w_in.shape[1]
    width = model_width // PARTS
    slab = CAP * PARTS
    group = math.gcd(n, 4)
    return pl.pallas_call(
        functools.partial(kernel, n, group),
        out_shape=jax.ShapeDtypeStruct((tok_dev, model_width), BF16),
        in_specs=[
            pl.BlockSpec(memory_space=pl.ANY),
            pl.BlockSpec(memory_space=pltpu.VMEM),
            pl.BlockSpec(memory_space=pl.ANY),
            pl.BlockSpec(memory_space=pltpu.VMEM),
            pl.BlockSpec(memory_space=pl.ANY),
        ],
        out_specs=pl.BlockSpec(memory_space=pltpu.VMEM),
        scratch_shapes=[
            pltpu.VMEM((PARTS * tok_dev, width), BF16),
            pltpu.VMEM((width, PARTS * neurons), BF16),
            pltpu.VMEM((PARTS * neurons, width), BF16),
            pltpu.VMEM((n, slab, width), BF16),
            pltpu.VMEM((n, slab, width), BF16),
            pltpu.VMEM((n, slab, width), BF16),
            pltpu.VMEM((n, slab, width), BF16),
            pltpu.VMEM((n * slab, PARTS * tok_dev), BF16),
            pltpu.VMEM((PARTS * tok_dev, width), F32),
            pltpu.SemaphoreType.DMA((3, PARTS)),
            pltpu.SemaphoreType.DMA((n,)),
            pltpu.SemaphoreType.DMA((n,)),
            pltpu.SemaphoreType.DMA((n,)),
            pltpu.SemaphoreType.DMA((n,)),
        ],
        compiler_params=pltpu.CompilerParams(
            collective_id=0, has_side_effects=True, vmem_limit_bytes=60 * 1024 * 1024),
    )(tokens, block_ids, w_in, bias_in.reshape(1, -1), w_out)


def solution(mesh):
    return jax.shard_map(
        body,
        mesh=mesh,
        in_specs=(
            P(("tok", "blk"), None),
            P(("tok", "blk"), None),
            P(None, "blk"),
            P("blk"),
            P("blk", None),
        ),
        out_specs=P(("tok", "blk"), None),
        check_vma=False,
    )
```

```python
import functools
import math

import jax
import jax.numpy as jnp
from jax import lax
from jax.experimental import pallas as pl
from jax.experimental.pallas import tpu as pltpu
from jax.sharding import PartitionSpec as P

CAP = 5
PARTS = 8
CHUNKS = 4
F32 = jnp.float32
BF16 = jnp.bfloat16


def iota(shape, dim):
    return lax.broadcasted_iota(jnp.int32, shape, dim)


def lookup(index, values):
    total = values[0]
    for at, value in enumerate(values):
        total = jnp.where(index == at, value, total)
    return total


def remote(src, dst, send, recv, target):
    return pltpu.make_async_remote_copy(
        src_ref=src, dst_ref=dst, send_sem=send, recv_sem=recv,
        device_id={"blk": target}, device_id_type=pl.DeviceIdType.MESH)


def kernel(
    outer, inner, tok_ref, ids_ref, w_in_ref, bias_ref, w_out_ref, out_ref,
    raw, ranks, win8, wout8, outgoing, incoming, result, returned, route, partial, above, below, acc,
    load_sem, raw_send, raw_recv, rank_send, rank_recv, fsend, frecv, bsend, brecv,
    part_send, above_recv, below_recv,
):
    me = lax.axis_index("blk")
    o, i0 = me // inner, me % inner
    last = outer - 1
    tok_dev, top = ids_ref.shape
    width = raw.shape[2]
    neurons = w_in_ref.shape[1]
    lanes = ranks.shape[2]
    slab = CAP * PARTS
    rows = inner * slab
    piece = PARTS * tok_dev // CHUNKS

    near = [sorted(range(outer), key=lambda s, a=a: (abs(s - a), s)) for a in range(outer)]
    ready = [sorted([s for s in range(outer) if s != a],
                    key=lambda s, a=a: (s + a if s > a else 2 * last - s - a, s))
             for a in range(outer)]
    source = [lookup(o, [near[a][t] for a in range(outer)]) for t in range(outer)]

    loads = []
    for h in range(PARTS):
        cols = pl.ds(h * width, width)
        loads.append(pltpu.make_async_copy(
            tok_ref.at[:, cols], raw.at[o, pl.ds(h * tok_dev, tok_dev)], load_sem.at[0, h]))
        loads.append(pltpu.make_async_copy(
            w_in_ref.at[cols], win8.at[:, pl.ds(h * neurons, neurons)], load_sem.at[1, h]))
        loads.append(pltpu.make_async_copy(
            w_out_ref.at[:, cols], wout8.at[pl.ds(h * neurons, neurons)], load_sem.at[2, h]))
    for copy in loads[0::3] + loads[1::3] + loads[2::3]:
        copy.start()

    column = [lax.rem(o + k, outer) * inner + i0 for k in range(outer)]
    ahead = [o * inner + lax.rem(i0 + k, inner) for k in range(inner)]
    behind = [o * inner + lax.rem(i0 - k + inner, inner) for k in range(inner)]
    barrier = pltpu.get_barrier_semaphore()
    for target in column[1:] + ahead[1:]:
        pl.semaphore_signal(barrier, inc=1, device_id={"blk": target},
                            device_id_type=pl.DeviceIdType.MESH)

    ids = ids_ref[...]
    block = iota((tok_dev, lanes), 1)
    member = jnp.zeros((tok_dev, lanes), F32)
    for k in range(top):
        member = member + (ids[:, k:k + 1] == block).astype(F32)
    lower = (iota((tok_dev, tok_dev), 1) < iota((tok_dev, tok_dev), 0)).astype(F32)
    rank = jnp.dot(lower, member, preferred_element_type=F32)
    ranks[o] = jnp.where(member > 0.5, rank, 99.0).astype(BF16)

    up = jnp.minimum(o + 1, last) * inner + i0
    down = jnp.maximum(o - 1, 0) * inner + i0

    def raw_copy(s, side):
        return remote(raw.at[s], raw.at[s], raw_send.at[side, s], raw_recv.at[s],
                      up if side == 0 else down)

    def rank_copy(k, s):
        return remote(ranks.at[s], ranks.at[s], rank_send.at[k], rank_recv.at[s], column[k])

    def out_copy(t, k):
        return remote(outgoing.at[t, k], incoming.at[t, k], fsend.at[t, k], frecv.at[t, k], ahead[k])

    def back_copy(t, k):
        return remote(result.at[t, k], returned.at[t, k], bsend.at[t, k], brecv.at[t, k], behind[k])

    def part_copy(s, c, side):
        span = pl.ds(c * piece, piece)
        land, recv = (below, below_recv) if side == 0 else (above, above_recv)
        return remote(partial.at[s, span], land.at[s, span], part_send.at[s, c], recv.at[s, c],
                      up if side == 0 else down)

    row = iota((rows, lanes), 0)
    pick = ((o * inner + (i0 + row // slab) % inner) == iota((rows, lanes), 1)).astype(BF16)
    r = iota((rows, PARTS * tok_dev), 0) % slab
    slot = (r % CAP).astype(F32)
    aligned = r // CAP == iota((rows, PARTS * tok_dev), 1) // tok_dev
    ra, rb = iota((rows, rows), 0), iota((rows, rows), 1)
    same = ((ra // slab == rb // slab) & (ra % CAP == rb % CAP)).astype(F32)
    part = (iota((rows, PARTS * neurons), 0) % slab // CAP) == (
        iota((rows, PARTS * neurons), 1) // neurons)

    def dispatch(t):
        s = source[t]
        if t > 0:
            raw_copy(s, 0).wait_recv()

        @pl.when((s <= o) & (o < last))
        def _():
            raw_copy(s, 0).start()

        @pl.when((s >= o) & (o > 0))
        def _():
            raw_copy(s, 1).start()

        if t == 0:
            for k in range(1, outer):
                rank_copy(k, o).start()
        else:
            rank_copy(0, s).wait_recv()
        rank8 = jnp.concatenate([ranks[s]] * PARTS, axis=0)
        place = lax.dot_general(pick, rank8, (((1,), (1,)), ((), ())), preferred_element_type=F32)
        chosen = ((jnp.abs(place - slot) < 0.5) & aligned).astype(BF16)
        route[t] = chosen
        packed = jnp.dot(chosen, raw[s], preferred_element_type=F32).astype(BF16)
        for k in range(inner):
            outgoing[t, k] = packed[k * slab:(k + 1) * slab]
        for k in range(1, inner):
            out_copy(t, k).start()

    def compute(t):
        for k in range(1, inner):
            out_copy(t, k).wait_recv()
        x = jnp.concatenate([outgoing[t, 0]] + [incoming[t, k] for k in range(1, inner)], axis=0)
        wide = jnp.where(part, jnp.dot(x, win8[...], preferred_element_type=F32), 0.0)
        own = wide[:, :neurons]
        for h in range(1, PARTS):
            own = own + wide[:, h * neurons:(h + 1) * neurons]
        pre = jnp.dot(same, own, preferred_element_type=F32, precision=lax.Precision.HIGHEST)
        hidden = jnp.maximum(pre + bias_ref[...], 0.0)
        hidden8 = jnp.where(part, jnp.concatenate([hidden] * PARTS, axis=1), 0.0).astype(BF16)
        back = jnp.dot(hidden8, wout8[...], preferred_element_type=F32).astype(BF16)
        for k in range(inner):
            result[t, k] = back[k * slab:(k + 1) * slab]
        for k in range(1, inner):
            back_copy(t, k).start()

    def pass_on(s, wait):
        for side in range(2):
            land, recv = (below, below_recv) if side == 0 else (above, above_recv)

            @pl.when((s > o) if side == 0 else (s < o))
            def _():
                for c in range(CHUNKS):
                    span = pl.ds(c * piece, piece)
                    if wait:
                        part_copy(s, c, side).wait_recv()
                        partial[s, span] = (
                            partial[s, span].astype(F32) + land[s, span].astype(F32)).astype(BF16)
                    part_copy(s, c, side).start()

    def combine(t):
        for k in range(1, inner):
            back_copy(t, k).wait_recv()
        y = jnp.concatenate([result[t, 0]] + [returned[t, k] for k in range(1, inner)], axis=0)
        total = lax.dot_general(route[t], y, (((0,), (0,)), ((), ())), preferred_element_type=F32)
        s = source[t]
        partial[s] = total.astype(BF16)
        if t > 0:
            @pl.when((o == 0) | (o == last))
            def _():
                pass_on(s, False)

    for copy in loads[0::3]:
        copy.wait()
    pl.semaphore_wait(barrier, outer + inner - 2)
    for t in range(outer + 2):
        if t < outer:
            dispatch(t)
        if t == 1:
            for copy in loads[1::3] + loads[2::3]:
                copy.wait()
        if 1 <= t <= outer:
            compute(t - 1)
        if t >= 2:
            combine(t - 2)

    for t in range(outer - 1):
        s = lookup(o, [ready[a][t] for a in range(outer)])

        @pl.when((o > 0) & (o < last))
        def _():
            pass_on(s, True)

    for c in range(CHUNKS):
        span = pl.ds(c * piece, piece)
        acc[...] = partial[o, span].astype(F32)

        @pl.when(o < last)
        def _():
            part_copy(o, c, 1).wait_recv()
            acc[...] += above[o, span].astype(F32)

        @pl.when(o > 0)
        def _():
            part_copy(o, c, 0).wait_recv()
            acc[...] += below[o, span].astype(F32)

        for j in range(PARTS // CHUNKS):
            h = c * (PARTS // CHUNKS) + j
            out_ref[:, h * width:(h + 1) * width] = (
                acc[j * tok_dev:(j + 1) * tok_dev].astype(BF16))

    for t in range(outer):
        s = source[t]

        @pl.when((s <= o) & (o < last))
        def _():
            raw_copy(s, 0).wait_send()

        @pl.when((s >= o) & (o > 0))
        def _():
            raw_copy(s, 1).wait_send()

        for k in range(1, inner):
            out_copy(t, k).wait_send()
            back_copy(t, k).wait_send()
        if t > 0:
            rank_copy(t, o).wait_send()
            for c in range(CHUNKS):
                part_copy(s, c, 0).wait_send()


def body(tokens, block_ids, w_in, bias_in, w_out):
    n = lax.axis_size("blk")
    tok_dev, model_width = tokens.shape
    neurons = w_in.shape[1]
    width = model_width // PARTS
    slab = CAP * PARTS
    inner = max(k for k in range(1, math.isqrt(n) + 1) if n % k == 0)
    outer = n // inner
    lanes = 128 * ((n + 127) // 128)
    lines = pltpu.VMEM((outer, PARTS * tok_dev, width), BF16)
    slabs = pltpu.VMEM((outer, inner, slab, width), BF16)
    dma = pltpu.SemaphoreType.DMA
    return pl.pallas_call(
        functools.partial(kernel, outer, inner),
        out_shape=jax.ShapeDtypeStruct((tok_dev, model_width), BF16),
        in_specs=[
            pl.BlockSpec(memory_space=pl.ANY),
            pl.BlockSpec(memory_space=pltpu.VMEM),
            pl.BlockSpec(memory_space=pl.ANY),
            pl.BlockSpec(memory_space=pltpu.VMEM),
            pl.BlockSpec(memory_space=pl.ANY),
        ],
        out_specs=pl.BlockSpec(memory_space=pltpu.VMEM),
        scratch_shapes=[
            lines,
            pltpu.VMEM((outer, tok_dev, lanes), BF16),
            pltpu.VMEM((width, PARTS * neurons), BF16),
            pltpu.VMEM((PARTS * neurons, width), BF16),
            slabs, slabs, slabs, slabs,
            pltpu.VMEM((outer, inner * slab, PARTS * tok_dev), BF16),
            lines, lines, lines,
            pltpu.VMEM((PARTS * tok_dev // CHUNKS, width), F32),
            dma((3, PARTS)),
            dma((2, outer)), dma((outer,)),
            dma((outer,)), dma((outer,)),
            dma((outer, inner)), dma((outer, inner)),
            dma((outer, inner)), dma((outer, inner)),
            dma((outer, CHUNKS)), dma((outer, CHUNKS)), dma((outer, CHUNKS)),
        ],
        compiler_params=pltpu.CompilerParams(
            collective_id=0, has_side_effects=True, vmem_limit_bytes=60 * 1024 * 1024),
    )(tokens, block_ids, w_in, bias_in.reshape(1, -1), w_out)


def solution(mesh):
    return jax.shard_map(
        body,
        mesh=mesh,
        in_specs=(
            P(("tok", "blk"), None),
            P(("tok", "blk"), None),
            P(None, "blk"),
            P("blk"),
            P("blk", None),
        ),
        out_specs=P(("tok", "blk"), None),
        check_vma=False,
    )
```

```python
import functools
import math

import jax
import jax.numpy as jnp
from jax import lax
from jax.experimental import pallas as pl
from jax.experimental.pallas import tpu as pltpu
from jax.sharding import PartitionSpec as P

CAP = 5
PARTS = 8
CHUNKS = 4
F32 = jnp.float32
BF16 = jnp.bfloat16


def iota(shape, dim):
    return lax.broadcasted_iota(jnp.int32, shape, dim)


def lookup(index, values):
    total = values[0]
    for at, value in enumerate(values):
        total = jnp.where(index == at, value, total)
    return total


def remote(src, dst, send, recv, target):
    return pltpu.make_async_remote_copy(
        src_ref=src, dst_ref=dst, send_sem=send, recv_sem=recv,
        device_id={"blk": target}, device_id_type=pl.DeviceIdType.MESH)


def kernel(
    outer, inner, tok_ref, ids_ref, w_in_ref, bias_ref, w_out_ref, out_ref,
    raw, ranks, win8, wout8, outgoing, incoming, result, returned, route, partial, above, below, acc,
    load_sem, raw_send, raw_recv, rank_send, rank_recv, fsend, frecv, bsend, brecv,
    part_send, above_recv, below_recv,
):
    me = lax.axis_index("blk")
    o, i0 = me // inner, me % inner
    last = outer - 1
    top, tok_dev = ids_ref.shape
    width = raw.shape[2]
    neurons = w_in_ref.shape[1]
    lanes = ranks.shape[2]
    slab = CAP * PARTS
    rows = inner * slab
    piece = PARTS * tok_dev // CHUNKS

    near = [sorted(range(outer), key=lambda s, a=a: (abs(s - a), s)) for a in range(outer)]
    ready = [sorted([s for s in range(outer) if s != a],
                    key=lambda s, a=a: (s + a if s > a else 2 * last - s - a, s))
             for a in range(outer)]
    source = [lookup(o, [near[a][t] for a in range(outer)]) for t in range(outer)]

    column = [lax.rem(o + k, outer) * inner + i0 for k in range(outer)]
    ahead = [o * inner + lax.rem(i0 + k, inner) for k in range(inner)]
    behind = [o * inner + lax.rem(i0 - k + inner, inner) for k in range(inner)]
    barrier = pltpu.get_barrier_semaphore()
    for target in column[1:] + ahead[1:]:
        pl.semaphore_signal(barrier, inc=1, device_id={"blk": target},
                            device_id_type=pl.DeviceIdType.MESH)

    loads = []
    for h in range(PARTS):
        cols = pl.ds(h * width, width)
        loads.append(pltpu.make_async_copy(
            tok_ref.at[:, cols], raw.at[o, pl.ds(h * tok_dev, tok_dev)], load_sem.at[0, h]))
        loads.append(pltpu.make_async_copy(
            w_in_ref.at[cols], win8.at[:, pl.ds(h * neurons, neurons)], load_sem.at[1, h]))
        loads.append(pltpu.make_async_copy(
            w_out_ref.at[:, cols], wout8.at[pl.ds(h * neurons, neurons)], load_sem.at[2, h]))
    for copy in loads[0::3] + loads[1::3] + loads[2::3]:
        copy.start()

    ids = ids_ref[...]
    block = iota((lanes, tok_dev), 0)
    member = jnp.zeros((lanes, tok_dev), F32)
    for k in range(top):
        member = member + (ids[k:k + 1, :] == block).astype(F32)
    earlier = (iota((tok_dev, tok_dev), 0) < iota((tok_dev, tok_dev), 1)).astype(F32)
    rank = jnp.dot(member, earlier, preferred_element_type=F32)
    rank = jnp.where(member > 0.5, rank, 99.0).astype(BF16)
    unit = (iota((lanes, lanes), 0) == iota((lanes, lanes), 1)).astype(BF16)
    ranks[o] = lax.dot_general(rank, unit, (((0,), (0,)), ((), ())),
                               preferred_element_type=F32).astype(BF16)

    up = jnp.minimum(o + 1, last) * inner + i0
    down = jnp.maximum(o - 1, 0) * inner + i0

    def raw_copy(s, side):
        return remote(raw.at[s], raw.at[s], raw_send.at[side, s], raw_recv.at[s],
                      up if side == 0 else down)

    def rank_copy(k, s):
        return remote(ranks.at[s], ranks.at[s], rank_send.at[k], rank_recv.at[s], column[k])

    def out_copy(t, k):
        return remote(outgoing.at[t, k], incoming.at[t, k], fsend.at[t, k], frecv.at[t, k], ahead[k])

    def back_copy(t, k):
        return remote(result.at[t, k], returned.at[t, k], bsend.at[t, k], brecv.at[t, k], behind[k])

    def part_copy(s, c, side):
        span = pl.ds(c * piece, piece)
        land, recv = (below, below_recv) if side == 0 else (above, above_recv)
        return remote(partial.at[s, span], land.at[s, span], part_send.at[s, c], recv.at[s, c],
                      up if side == 0 else down)

    row = iota((rows, lanes), 0)
    pick = ((o * inner + (i0 + row // slab) % inner) == iota((rows, lanes), 1)).astype(BF16)
    r = iota((rows, PARTS * tok_dev), 0) % slab
    slot = (r % CAP).astype(F32)
    aligned = r // CAP == iota((rows, PARTS * tok_dev), 1) // tok_dev
    ra, rb = iota((rows, rows), 0), iota((rows, rows), 1)
    same = ((ra // slab == rb // slab) & (ra % CAP == rb % CAP)).astype(F32)
    part = (iota((rows, PARTS * neurons), 0) % slab // CAP) == (
        iota((rows, PARTS * neurons), 1) // neurons)

    inside = (o > 0) & (o < last)

    def relay(t):
        @pl.when(inside)
        def _():
            s = source[t]
            raw_copy(s, 0).wait_recv()

            @pl.when(s < o)
            def _():
                raw_copy(s, 0).start()

            @pl.when(s > o)
            def _():
                raw_copy(s, 1).start()

    def dispatch(t):
        s = source[t]
        if t == 0:
            @pl.when(o < last)
            def _():
                raw_copy(o, 0).start()

            @pl.when(o > 0)
            def _():
                raw_copy(o, 1).start()

            for k in range(1, outer):
                rank_copy(k, o).start()
        else:
            @pl.when(jnp.logical_not(inside))
            def _():
                raw_copy(s, 0).wait_recv()

            rank_copy(0, s).wait_recv()
        rank8 = jnp.concatenate([ranks[s]] * PARTS, axis=0)
        place = lax.dot_general(pick, rank8, (((1,), (1,)), ((), ())), preferred_element_type=F32)
        chosen = ((jnp.abs(place - slot) < 0.5) & aligned).astype(BF16)
        route[t] = chosen
        packed = jnp.dot(chosen, raw[s], preferred_element_type=F32).astype(BF16)
        for k in range(inner):
            outgoing[t, k] = packed[k * slab:(k + 1) * slab]
        for k in range(1, inner):
            out_copy(t, k).start()

    def compute(t):
        for k in range(1, inner):
            out_copy(t, k).wait_recv()
        x = jnp.concatenate([outgoing[t, 0]] + [incoming[t, k] for k in range(1, inner)], axis=0)
        wide = jnp.where(part, jnp.dot(x, win8[...], preferred_element_type=F32), 0.0)
        own = wide[:, :neurons]
        for h in range(1, PARTS):
            own = own + wide[:, h * neurons:(h + 1) * neurons]
        pre = jnp.dot(same, own, preferred_element_type=F32, precision=lax.Precision.HIGHEST)
        hidden = jnp.maximum(pre + bias_ref[...], 0.0)
        hidden8 = jnp.where(part, jnp.concatenate([hidden] * PARTS, axis=1), 0.0).astype(BF16)
        back = jnp.dot(hidden8, wout8[...], preferred_element_type=F32).astype(BF16)
        for k in range(inner):
            result[t, k] = back[k * slab:(k + 1) * slab]
        for k in range(1, inner):
            back_copy(t, k).start()

    def pass_on(s, wait):
        for side in range(2):
            land, recv = (below, below_recv) if side == 0 else (above, above_recv)

            @pl.when((s > o) if side == 0 else (s < o))
            def _():
                for c in range(CHUNKS):
                    span = pl.ds(c * piece, piece)
                    if wait:
                        part_copy(s, c, side).wait_recv()
                        partial[s, span] = (
                            partial[s, span].astype(F32) + land[s, span].astype(F32)).astype(BF16)
                    part_copy(s, c, side).start()

    def combine(t):
        for k in range(1, inner):
            back_copy(t, k).wait_recv()
        y = jnp.concatenate([result[t, 0]] + [returned[t, k] for k in range(1, inner)], axis=0)
        total = lax.dot_general(route[t], y, (((0,), (0,)), ((), ())), preferred_element_type=F32)
        s = source[t]
        partial[s] = total.astype(BF16)
        if t > 0:
            @pl.when(jnp.logical_not(inside))
            def _():
                pass_on(s, False)

    for copy in loads[0::3]:
        copy.wait()
    pl.semaphore_wait(barrier, outer + inner - 2)
    for t in range(outer + 2):
        if 0 < t < outer:
            relay(t)
        if t < outer:
            dispatch(t)
        if t == 0:
            for copy in loads[1::3] + loads[2::3]:
                copy.wait()
        if 1 <= t <= outer:
            compute(t - 1)
        if t >= 2:
            combine(t - 2)

    for t in range(outer - 1):
        s = lookup(o, [ready[a][t] for a in range(outer)])

        @pl.when(inside)
        def _():
            pass_on(s, True)

    for c in range(CHUNKS):
        span = pl.ds(c * piece, piece)
        acc[...] = partial[o, span].astype(F32)

        @pl.when(o < last)
        def _():
            part_copy(o, c, 1).wait_recv()
            acc[...] += above[o, span].astype(F32)

        @pl.when(o > 0)
        def _():
            part_copy(o, c, 0).wait_recv()
            acc[...] += below[o, span].astype(F32)

        for j in range(PARTS // CHUNKS):
            h = c * (PARTS // CHUNKS) + j
            out_ref[:, h * width:(h + 1) * width] = (
                acc[j * tok_dev:(j + 1) * tok_dev].astype(BF16))

    for t in range(outer):
        s = source[t]

        @pl.when((s <= o) & (o < last))
        def _():
            raw_copy(s, 0).wait_send()

        @pl.when((s >= o) & (o > 0))
        def _():
            raw_copy(s, 1).wait_send()

        for k in range(1, inner):
            out_copy(t, k).wait_send()
            back_copy(t, k).wait_send()
        if t > 0:
            rank_copy(t, o).wait_send()
            for c in range(CHUNKS):
                part_copy(s, c, 0).wait_send()


def body(tokens, block_ids, w_in, bias_in, w_out):
    n = lax.axis_size("blk")
    tok_dev, model_width = tokens.shape
    neurons = w_in.shape[1]
    width = model_width // PARTS
    slab = CAP * PARTS
    inner = max(k for k in range(1, math.isqrt(n) + 1) if n % k == 0)
    outer = n // inner
    lanes = 128 * ((n + 127) // 128)
    lines = pltpu.VMEM((outer, PARTS * tok_dev, width), BF16)
    slabs = pltpu.VMEM((outer, inner, slab, width), BF16)
    dma = pltpu.SemaphoreType.DMA
    return pl.pallas_call(
        functools.partial(kernel, outer, inner),
        out_shape=jax.ShapeDtypeStruct((tok_dev, model_width), BF16),
        in_specs=[
            pl.BlockSpec(memory_space=pl.ANY),
            pl.BlockSpec(memory_space=pltpu.VMEM),
            pl.BlockSpec(memory_space=pl.ANY),
            pl.BlockSpec(memory_space=pltpu.VMEM),
            pl.BlockSpec(memory_space=pl.ANY),
        ],
        out_specs=pl.BlockSpec(memory_space=pltpu.VMEM),
        scratch_shapes=[
            lines,
            pltpu.VMEM((outer, tok_dev, lanes), BF16),
            pltpu.VMEM((width, PARTS * neurons), BF16),
            pltpu.VMEM((PARTS * neurons, width), BF16),
            slabs, slabs, slabs, slabs,
            pltpu.VMEM((outer, inner * slab, PARTS * tok_dev), BF16),
            lines, lines, lines,
            pltpu.VMEM((PARTS * tok_dev // CHUNKS, width), F32),
            dma((3, PARTS)),
            dma((2, outer)), dma((outer,)),
            dma((outer,)), dma((outer,)),
            dma((outer, inner)), dma((outer, inner)),
            dma((outer, inner)), dma((outer, inner)),
            dma((outer, CHUNKS)), dma((outer, CHUNKS)), dma((outer, CHUNKS)),
        ],
        compiler_params=pltpu.CompilerParams(
            collective_id=0, has_side_effects=True, vmem_limit_bytes=60 * 1024 * 1024),
    )(tokens, block_ids.T, w_in, bias_in.reshape(1, -1), w_out)


def solution(mesh):
    return jax.shard_map(
        body,
        mesh=mesh,
        in_specs=(
            P(("tok", "blk"), None),
            P(("tok", "blk"), None),
            P(None, "blk"),
            P("blk"),
            P("blk", None),
        ),
        out_specs=P(("tok", "blk"), None),
        check_vma=False,
    )
```
